32 devices in a mesh: row: 8 (over y, x, core), col: 4 (over z).
Axes of the slice: x: 2, y: 2, z: 4, core: 2. Of those that a mesh axis runs over, the one named last changes fastest.
Arguments:
- matrix: bfloat16 [16384, 8192], P('row', 'col'), may hold values from 0 to 1
- labels: int32 [16384, 1], P('row'), may hold values from 0 to 7
- root_rows: float32 [8, 16384], P(None, 'row'), may hold values from 0.2 to 1
- root_cols: float32 [8, 8192], P(None, 'col'), may hold values from 0.2 to 1
- child_rows: float32 [16, 16384], P(None, 'row'), may hold values from 0.2 to 1
- child_cols: float32 [128, 8192], P(None, 'col'), may hold values from 0.2 to 1
Outputs:
- root_w: float32 [8, 16384], P(None, 'row')
- root_h: float32 [8, 8192], P(None, 'col')
- child_w: float32 [16, 16384], P(None, 'row')
- child_h: float32 [128, 8192], P(None, 'col')
The draws below stay inside these ranges and needn't reach their ends.
Inputs may be any that keep to these rules, and one draw needn't show every extreme that they name: `labels`: every cluster 0 to 7 holds at least one node.
All inputs are finite; a program needn't handle non-finite values.
Results may differ from the reference program's by a relative error of at most 0.00035.
Values sent between devices are 32-bit elements; how exact they have to be, the bound alone decides.
No kernel may reach another device: no remote copies, remote signals or barrier semaphores. Data moves between devices by JAX's collectives and lax.ppermute only.
A program may use at most 64 MiB of HBM per device.

```python
import jax
import jax.numpy as jnp
from jax import lax

BINS = 8192
K_ROOT = 8
K_CHILD = 16
CHILDREN = 8
ROOT_ITERS = 2
CHILD_ITERS = 3
NODES = 16384


def shard_levels(rng, shape, split, least, high):
    gain = 1.0
    for position, parts in split:
        heights = jax.random.uniform(jax.random.fold_in(jax.random.fold_in(rng, 6), position), (parts,), jnp.float32, least / len(split), high / len(split))
        gain = gain * jnp.repeat(jnp.exp(heights), shape[position] // parts).reshape((-1,) + (1,) * (len(shape) - 1 - position))
    return gain


def choose_distinct(own_key, rows, amount, top, lift):
    sequence = jax.random.permutation(jax.random.fold_in(own_key, 1), amount)
    boost = sequence
    for power in range(3):
        boost = boost * boost // amount
    boost = boost * lift // amount
    lots = jax.random.randint(jax.random.fold_in(own_key, 2), (rows, amount), 0, 4096) + boost
    holders = jax.random.permutation(jax.random.fold_in(own_key, 3), rows)[jnp.arange(amount) % rows]
    lots = jnp.where(jnp.arange(rows)[:, None] == holders[None, :], 1 << 14, lots)
    priority = lots * amount + jnp.arange(amount)
    return lax.top_k(priority.astype(jnp.int32), top)[1].astype(jnp.int32)


def setup_inputs(seed: int = 0) -> dict:
    seeds = jax.random.split(jax.random.key(seed), 7)
    return {
        "matrix": jnp.clip(1.0 * jax.random.uniform(seeds[0], (NODES, BINS), jnp.float32) ** shard_levels(seeds[0], (NODES, BINS), ((0, 8), (1, 4)), -0.2, 0.2), 0.0, 1.0).astype(jnp.bfloat16),
        "labels": choose_distinct(seeds[1], NODES, CHILDREN, 1, 2048),
        "root_rows": jnp.clip(0.2 + 0.8 * jax.random.uniform(seeds[2], (K_ROOT, NODES), jnp.float32) ** shard_levels(seeds[2], (K_ROOT, NODES), ((1, 8),), -0.2, 0.2), 0.2, 1.0),
        "root_cols": jnp.clip(0.2 + 0.8 * jax.random.uniform(seeds[3], (K_ROOT, BINS), jnp.float32) ** shard_levels(seeds[3], (K_ROOT, BINS), ((1, 4),), -0.2, 0.2), 0.2, 1.0),
        "child_rows": jnp.clip(0.2 + 0.8 * jax.random.uniform(seeds[4], (K_CHILD, NODES), jnp.float32) ** shard_levels(seeds[4], (K_CHILD, NODES), ((1, 8),), -0.2, 0.2), 0.2, 1.0),
        "child_cols": jnp.clip(0.2 + 0.8 * jax.random.uniform(seeds[5], (CHILDREN * K_CHILD, BINS), jnp.float32) ** shard_levels(seeds[5], (CHILDREN * K_CHILD, BINS), ((1, 4),), -0.2, 0.2), 0.2, 1.0),
    }


HIGH = lax.Precision.HIGHEST


def times_transpose(left_bf, matrix):
    return lax.dot_general(left_bf, matrix, (((1,), (1,)), ((), ())), preferred_element_type=jnp.float32)


def reference(matrix, labels, root_rows, root_cols, child_rows, child_cols):
    root_w = root_rows
    root_h = root_cols
    for iteration in range(ROOT_ITERS):
        numer_h = jnp.dot(root_w.astype(jnp.bfloat16), matrix, preferred_element_type=jnp.float32)
        gram_w = jnp.dot(root_w, root_w.T, precision=HIGH)
        root_h = root_h * numer_h / jnp.dot(gram_w, root_h, precision=HIGH)
        numer_w = times_transpose(root_h.astype(jnp.bfloat16), matrix)
        gram_h = jnp.dot(root_h, root_h.T, precision=HIGH)
        root_w = root_w * numer_w / jnp.dot(gram_h, root_w, precision=HIGH)
    member = (labels[:, 0][None, :] == jnp.arange(CHILDREN, dtype=jnp.int32)[:, None]).astype(jnp.float32)
    own_weight = jnp.sum(member * root_w, axis=0)
    child_w = child_rows * own_weight[None, :]
    child_h = child_cols * jnp.repeat(root_h, K_CHILD, axis=0)
    for iteration in range(CHILD_ITERS):
        spread = member[:, None, :] * child_w[None, :, :]
        spread_bf = spread.reshape(CHILDREN * K_CHILD, -1).astype(jnp.bfloat16)
        numer_ch = jnp.dot(spread_bf, matrix, preferred_element_type=jnp.float32)
        gram_c = jnp.einsum('cjr,ckr->cjk', spread, spread, precision=HIGH)
        blocks = child_h.reshape(CHILDREN, K_CHILD, -1)
        lower = jnp.einsum('cjk,ckn->cjn', gram_c, blocks, precision=HIGH).reshape(CHILDREN * K_CHILD, -1)
        child_h = child_h * numer_ch / lower
        full_rows = times_transpose(child_h.astype(jnp.bfloat16), matrix)
        numer_cw = jnp.sum(full_rows.reshape(CHILDREN, K_CHILD, -1) * member[:, None, :], axis=0)
        blocks = child_h.reshape(CHILDREN, K_CHILD, -1)
        hgram = jnp.einsum('cjn,ckn->cjk', blocks, blocks, precision=HIGH)
        lower_w = jnp.sum(jnp.einsum('cjk,kr->cjr', hgram, child_w, precision=HIGH) * member[:, None, :], axis=0)
        child_w = child_w * numer_cw / lower_w
    return root_w, root_h, child_w, child_h
```

```python
import jax
import jax.numpy as jnp
from jax import lax
from jax.sharding import PartitionSpec as P

K_CHILD = 16
CHILDREN = 8
ROOT_ITERS = 2
CHILD_ITERS = 3


HIGH = lax.Precision.HIGHEST


def times_transpose(left_bf, matrix):
    return lax.dot_general(
        left_bf, matrix, (((1,), (1,)), ((), ())), preferred_element_type=jnp.float32
    )


def swap(x, axis, size, mask):
    return lax.ppermute(x, axis, [(i, i ^ mask) for i in range(size)])


def masks_of(size):
    return [1 << b for b in range(size.bit_length() - 1)]


def butterfly(x, axis, size, masks):
    masks = list(masks)
    while masks:
        if len(masks) == 1:
            x = x + swap(x, axis, size, masks.pop(0))
            continue
        a, b = masks.pop(0), masks.pop(0)
        xa, xb, xab = (swap(x, axis, size, m) for m in (a, b, a ^ b))
        x = (x + xa) + (xb + xab)
    return x


def sum_rows(x, rows):
    masks = masks_of(rows)
    x = x + swap(x, "row", rows, 1)
    return butterfly(x, "row", rows, masks[1:])


def sum_cols(x, cols):
    return butterfly(x, "col", cols, masks_of(cols))


def make_body(rows, cols):
    def body(matrix, labels, root_rows, root_cols, child_rows, child_cols):
        root_w = root_rows
        root_h = root_cols
        for iteration in range(ROOT_ITERS):
            gram_w = sum_rows(jnp.dot(root_w, root_w.T, precision=HIGH), rows)
            numer_h = jnp.dot(root_w.astype(jnp.bfloat16), matrix, preferred_element_type=jnp.float32)
            numer_h = sum_rows(numer_h, rows)
            root_h = root_h * numer_h / jnp.dot(gram_w, root_h, precision=HIGH)
            gram_h = sum_cols(jnp.dot(root_h, root_h.T, precision=HIGH), cols)
            numer_w = times_transpose(root_h.astype(jnp.bfloat16), matrix)
            numer_w = sum_cols(numer_w, cols)
            root_w = root_w * numer_w / jnp.dot(gram_h, root_w, precision=HIGH)
        member = (labels[:, 0][None, :] == jnp.arange(CHILDREN, dtype=jnp.int32)[:, None]).astype(
            jnp.float32
        )
        own_weight = jnp.sum(member * root_w, axis=0)
        child_w = child_rows * own_weight[None, :]
        total_rows = CHILDREN * K_CHILD
        half = total_rows // 2
        core = lax.axis_index("row") & 1
        child_h = child_cols * jnp.repeat(root_h, K_CHILD, axis=0)
        mine = lax.dynamic_slice_in_dim(child_h, core * half, half, 0)
        masks = masks_of(rows)[1:]
        for iteration in range(CHILD_ITERS):
            spread = member[:, None, :] * child_w[None, :, :]
            spread_bf = spread.reshape(total_rows, -1).astype(jnp.bfloat16)
            gram_c = sum_rows(jnp.einsum("cjr,ckr->cjk", spread, spread, precision=HIGH), rows)
            gram_mine = lax.dynamic_slice_in_dim(gram_c, core * (CHILDREN // 2), CHILDREN // 2, 0)
            blocks = mine.reshape(CHILDREN // 2, K_CHILD, -1)
            lower = jnp.einsum("cjk,ckn->cjn", gram_mine, blocks, precision=HIGH).reshape(half, -1)
            numer_ch = jnp.dot(spread_bf, matrix, preferred_element_type=jnp.float32)
            keep = lax.dynamic_slice_in_dim(numer_ch, core * half, half, 0)
            send = lax.dynamic_slice_in_dim(numer_ch, (1 - core) * half, half, 0)
            part = keep + swap(send, "row", rows, 1)
            first, second = part[: half // 2], part[half // 2 :]
            for a, b in zip(masks, masks[::-1]):
                first, second = (
                    first + swap(first, "row", rows, a),
                    second + swap(second, "row", rows, b),
                )
            mine = mine * jnp.concatenate([first, second]) / lower
            other = swap(mine, "row", rows, 1)
            low, high = jnp.where(core == 0, mine, other), jnp.where(core == 0, other, mine)
            child_h = jnp.concatenate([low, high])
            blocks = child_h.reshape(CHILDREN, K_CHILD, -1)
            hgram = sum_cols(jnp.einsum("cjn,ckn->cjk", blocks, blocks, precision=HIGH), cols)
            full_rows = times_transpose(child_h.astype(jnp.bfloat16), matrix)
            numer_cw = jnp.sum(full_rows.reshape(CHILDREN, K_CHILD, -1) * member[:, None, :], axis=0)
            numer_cw = sum_cols(numer_cw, cols)
            lower_w = jnp.sum(
                jnp.einsum("cjk,kr->cjr", hgram, child_w, precision=HIGH) * member[:, None, :], axis=0
            )
            child_w = child_w * numer_cw / lower_w
        return (root_w, root_h, child_w, child_h)

    return body


def solution(mesh):
    return jax.shard_map(
        make_body(mesh.shape["row"], mesh.shape["col"]),
        mesh=mesh,
        in_specs=(
            P("row", "col"),
            P("row", None),
            P(None, "row"),
            P(None, "col"),
            P(None, "row"),
            P(None, "col"),
        ),
        out_specs=(P(None, "row"), P(None, "col"), P(None, "row"), P(None, "col")),
        check_vma=False,
    )
```

```python
import jax
import jax.numpy as jnp
from jax import lax
from jax.sharding import PartitionSpec as P

K_CHILD = 16
CHILDREN = 8
ROOT_ITERS = 2
CHILD_ITERS = 3
LANES = 128
TOTAL = CHILDREN * K_CHILD

HIGH = lax.Precision.HIGHEST


def times_transpose(left_bf, matrix):
    return lax.dot_general(
        left_bf, matrix, (((1,), (1,)), ((), ())), preferred_element_type=jnp.float32
    )


def outer(a, b):
    return lax.dot_general(
        a, b, (((1,), (1,)), ((), ())), precision=HIGH, preferred_element_type=jnp.float32
    )


def swap(x, axis, size, mask):
    return lax.ppermute(x, axis, [(i, i ^ mask) for i in range(size)])


def masks_of(size):
    return [1 << b for b in range(size.bit_length() - 1)]


def butterfly(x, axis, size, masks):
    masks = list(masks)
    while masks:
        if len(masks) == 1:
            x = x + swap(x, axis, size, masks.pop(0))
            continue
        a, b = masks.pop(0), masks.pop(0)
        xa, xb, xab = (swap(x, axis, size, m) for m in (a, b, a ^ b))
        x = (x + xa) + (xb + xab)
    return x


def crossing(first, second, axis, size, masks):
    for a, b in zip(masks, masks[::-1]):
        first, second = (
            first + swap(first, axis, size, a),
            second + swap(second, axis, size, b),
        )
    return first, second


def pad_lanes(x):
    return jnp.pad(x, ((0, 0), (0, LANES - x.shape[1])))


def make_body(rows, cols):
    row_masks, col_masks = masks_of(rows), masks_of(cols)

    def sum_rows(x):
        x = x + swap(x, "row", rows, 1)
        return butterfly(x, "row", rows, row_masks[1:])

    def sum_cols(x):
        return butterfly(x, "col", cols, col_masks)

    def body(matrix, labels, root_rows, root_cols, child_rows, child_cols):
        odd = jnp.broadcast_to(lax.axis_index("row") & 1, (8, LANES))
        odd, root_rows = lax.optimization_barrier((odd, root_rows))
        is_odd = odd[:1, :1] == 1
        nodes, bins = matrix.shape
        k_root = root_rows.shape[0]

        def round_root(own, numer, reduce, width):
            packed = jnp.concatenate([numer, pad_lanes(outer(own, own))], axis=1)
            packed = reduce(packed)
            return packed[:, :width], packed[:, width : width + k_root]

        root_w, root_h = root_rows, root_cols
        for iteration in range(ROOT_ITERS):
            numer = jnp.dot(root_w.astype(jnp.bfloat16), matrix, preferred_element_type=jnp.float32)
            numer, gram = round_root(root_w, numer, sum_rows, bins)
            root_h = root_h * numer / jnp.dot(gram, root_h, precision=HIGH)
            numer = times_transpose(root_h.astype(jnp.bfloat16), matrix)
            numer, gram = round_root(root_h, numer, sum_cols, nodes)
            root_w = root_w * numer / jnp.dot(gram, root_w, precision=HIGH)

        member = (labels[:, 0][None, :] == jnp.arange(CHILDREN, dtype=jnp.int32)[:, None]).astype(
            jnp.float32
        )
        child_w = child_rows * jnp.sum(member * root_w, axis=0)[None, :]
        child_h = child_cols * jnp.repeat(root_h, K_CHILD, axis=0)
        quarter = TOTAL // 4
        pieces = [child_h[i * quarter : (i + 1) * quarter] for i in range(4)]
        mine = [jnp.where(is_odd, pieces[i + 2], pieces[i]) for i in range(2)]
        same = (
            jnp.arange(TOTAL, dtype=jnp.int32)[None, :] // K_CHILD
            == jnp.arange(CHILDREN, dtype=jnp.int32)[:, None]
        ).astype(jnp.float32)
        for iteration in range(CHILD_ITERS):
            spread = (member[:, None, :] * child_w[None, :, :]).reshape(TOTAL, nodes)
            gram = outer(spread, child_w)
            numer = jnp.dot(spread.astype(jnp.bfloat16), matrix, preferred_element_type=jnp.float32)
            packed = jnp.concatenate([numer, pad_lanes(gram)], axis=1)
            pieces = [packed[i * quarter : (i + 1) * quarter] for i in range(4)]
            parts = []
            for i in range(2):
                keep = jnp.where(is_odd, pieces[i + 2], pieces[i])
                send = jnp.where(is_odd, pieces[i], pieces[i + 2])
                parts.append(keep + swap(send, "row", rows, 1))
            parts = crossing(*parts, "row", rows, row_masks[1:])
            low, high = [], []
            for i in range(2):
                gram = parts[i][:, bins : bins + K_CHILD].reshape(-1, K_CHILD, K_CHILD)
                blocks = mine[i].reshape(-1, K_CHILD, bins)
                lower = jnp.einsum("cjk,ckn->cjn", gram, blocks, precision=HIGH).reshape(quarter, bins)
                mine[i] = mine[i] * parts[i][:, :bins] / lower
                other = swap(mine[i], "row", rows, 1)
                low.append(jnp.where(is_odd, other, mine[i]))
                high.append(jnp.where(is_odd, mine[i], other))
            child_h = jnp.concatenate(low + high)
            full = outer(child_h, child_h).reshape(CHILDREN, K_CHILD, TOTAL)
            gram = jnp.sum(full * same[:, None, :], axis=0)
            numer = times_transpose(child_h.astype(jnp.bfloat16), matrix)
            numer = jnp.sum(numer.reshape(CHILDREN, K_CHILD, nodes) * member[:, None, :], axis=0)
            packed = jnp.concatenate([numer, gram], axis=1)
            half = K_CHILD // 2
            packed = jnp.concatenate(crossing(packed[:half], packed[half:], "col", cols, col_masks))
            lower = jnp.dot(packed[:, nodes:], spread, precision=HIGH)
            child_w = child_w * packed[:, :nodes] / lower
        return (root_w, root_h, child_w, child_h)

    return body


def solution(mesh):
    return jax.shard_map(
        make_body(mesh.shape["row"], mesh.shape["col"]),
        mesh=mesh,
        in_specs=(
            P("row", "col"),
            P("row", None),
            P(None, "row"),
            P(None, "col"),
            P(None, "row"),
            P(None, "col"),
        ),
        out_specs=(P(None, "row"), P(None, "col"), P(None, "row"), P(None, "col")),
        check_vma=False,
    )
```

```python
import jax
import jax.numpy as jnp
from jax import lax
from jax.sharding import PartitionSpec as P

K_CHILD = 16
CHILDREN = 8
ROOT_ITERS = 2
CHILD_ITERS = 3
LANES = 128
TOTAL = CHILDREN * K_CHILD

HIGH = lax.Precision.HIGH


def times_transpose(left_bf, matrix):
    return lax.dot_general(
        left_bf, matrix, (((1,), (1,)), ((), ())), preferred_element_type=jnp.float32
    )


def outer(a, b):
    return lax.dot_general(
        a, b, (((1,), (1,)), ((), ())), precision=HIGH, preferred_element_type=jnp.float32
    )


def swap(x, axis, size, mask):
    return lax.ppermute(x, axis, [(i, i ^ mask) for i in range(size)])


def masks_of(size):
    return [1 << b for b in range(size.bit_length() - 1)]


def butterfly(x, axis, size, masks):
    masks = list(masks)
    while masks:
        if len(masks) == 1:
            x = x + swap(x, axis, size, masks.pop(0))
            continue
        a, b = masks.pop(0), masks.pop(0)
        xa, xb, xab = (swap(x, axis, size, m) for m in (a, b, a ^ b))
        x = (x + xa) + (xb + xab)
    return x


def crossing(parts, axis, size, masks):
    parts = list(parts)
    orders = [masks, masks[::-1]]
    for step in range(len(masks)):
        for i in range(len(parts)):
            parts[i] = parts[i] + swap(parts[i], axis, size, orders[i % 2][step])
    return parts


def pad_lanes(x):
    return jnp.pad(x, ((0, 0), (0, LANES - x.shape[1])))


def make_body(rows, cols):
    row_masks, col_masks = masks_of(rows), masks_of(cols)

    def sum_rows(x):
        x = x + swap(x, "row", rows, 1)
        return butterfly(x, "row", rows, row_masks[1:])

    def sum_cols(x):
        return butterfly(x, "col", cols, col_masks)

    def body(matrix, labels, root_rows, root_cols, child_rows, child_cols):
        odd = jnp.broadcast_to(lax.axis_index("row") & 1, (8, LANES))
        odd, root_rows = lax.optimization_barrier((odd, root_rows))
        is_odd = odd[:1, :1] == 1
        nodes, bins = matrix.shape
        k_root = root_rows.shape[0]

        def round_root(own, numer, reduce, width):
            packed = jnp.concatenate([numer, pad_lanes(outer(own, own))], axis=1)
            packed = reduce(packed)
            return packed[:, :width], packed[:, width : width + k_root]

        root_w, root_h = root_rows, root_cols
        for iteration in range(ROOT_ITERS):
            numer = jnp.dot(root_w.astype(jnp.bfloat16), matrix, preferred_element_type=jnp.float32)
            numer, gram = round_root(root_w, numer, sum_rows, bins)
            root_h = root_h * numer / jnp.dot(gram, root_h, precision=HIGH)
            numer = times_transpose(root_h.astype(jnp.bfloat16), matrix)
            numer, gram = round_root(root_h, numer, sum_cols, nodes)
            root_w = root_w * numer / jnp.dot(gram, root_w, precision=HIGH)

        member = (labels[:, 0][None, :] == jnp.arange(CHILDREN, dtype=jnp.int32)[:, None]).astype(
            jnp.float32
        )
        child_w = child_rows * jnp.sum(member * root_w, axis=0)[None, :]
        child_h = child_cols * jnp.repeat(root_h, K_CHILD, axis=0)
        parts_each = CHILDREN // 2
        size = TOTAL // CHILDREN
        pieces = [child_h[i * size : (i + 1) * size] for i in range(CHILDREN)]
        mine = [jnp.where(is_odd, pieces[i + parts_each], pieces[i]) for i in range(parts_each)]
        same = (
            jnp.arange(TOTAL, dtype=jnp.int32)[None, :] // K_CHILD
            == jnp.arange(CHILDREN, dtype=jnp.int32)[:, None]
        ).astype(jnp.float32)
        for iteration in range(CHILD_ITERS):
            spread = (member[:, None, :] * child_w[None, :, :]).reshape(TOTAL, nodes)
            gram = outer(spread, child_w)
            numer = jnp.dot(spread.astype(jnp.bfloat16), matrix, preferred_element_type=jnp.float32)
            packed = jnp.concatenate([numer, pad_lanes(gram)], axis=1)
            pieces = [packed[i * size : (i + 1) * size] for i in range(CHILDREN)]
            parts = []
            for i in range(parts_each):
                keep = jnp.where(is_odd, pieces[i + parts_each], pieces[i])
                send = jnp.where(is_odd, pieces[i], pieces[i + parts_each])
                parts.append(keep + swap(send, "row", rows, 1))
            parts = crossing(parts, "row", rows, row_masks[1:])
            low, high = [], []
            for i in range(parts_each):
                gram = parts[i][:, bins : bins + K_CHILD]
                lower = jnp.dot(gram, mine[i], precision=HIGH)
                mine[i] = mine[i] * parts[i][:, :bins] / lower
                tiled = jnp.concatenate([mine[i]] * CHILDREN)
                packed = jnp.concatenate([mine[i], outer(mine[i], tiled)], axis=1)
                other = swap(packed, "row", rows, 1)
                low.append(jnp.where(is_odd, other, packed))
                high.append(jnp.where(is_odd, packed, other))
            child_h = jnp.concatenate([x[:, :bins] for x in low + high])
            gram = sum(x[:, bins:] * same[c : c + 1] for c, x in enumerate(low + high))
            numer = times_transpose(child_h.astype(jnp.bfloat16), matrix)
            numer = jnp.sum(numer.reshape(CHILDREN, K_CHILD, nodes) * member[:, None, :], axis=0)
            packed = jnp.concatenate([numer, gram], axis=1)
            half = K_CHILD // 2
            packed = jnp.concatenate(crossing([packed[:half], packed[half:]], "col", cols, col_masks))
            lower = jnp.dot(packed[:, nodes:], spread, precision=HIGH)
            child_w = child_w * packed[:, :nodes] / lower
        return (root_w, root_h, child_w, child_h)

    return body


def solution(mesh):
    return jax.shard_map(
        make_body(mesh.shape["row"], mesh.shape["col"]),
        mesh=mesh,
        in_specs=(
            P("row", "col"),
            P("row", None),
            P(None, "row"),
            P(None, "col"),
            P(None, "row"),
            P(None, "col"),
        ),
        out_specs=(P(None, "row"), P(None, "col"), P(None, "row"), P(None, "col")),
        check_vma=False,
    )
```
